32 devices in a mesh: groups: 2 (over x), ctx: 16 (over z, y, core).
Axes of the slice: x: 2, y: 2, z: 4, core: 2. Of those that a mesh axis runs over, the one named last changes fastest.
Arguments:
- queries: bfloat16 [16384, 4096], P(('groups', 'ctx')), parts along dimension 0, may hold values from -50 to 50
- keys: bfloat16 [16384, 512], P(('groups', 'ctx')), parts along dimension 0, may hold values from -6 to 6
- values: bfloat16 [16384, 512], P(('groups', 'ctx')), parts along dimension 0, may hold values from -6 to 6
- doc_lengths: int32 [16], P('groups'), parts along dimension 0, may hold values from 1 to 2048, 8192 in all
Outputs:
- attended: bfloat16 [16384, 4096], P(('groups', 'ctx')), parts along dimension 0
The draws below stay inside these ranges and needn't reach their ends.
There are 2 independent parts, one for each index of `groups`. The reference program is written for one: setup_inputs(seed, part) draws one part's arguments, and reference() takes and returns one part's arrays. A program takes and returns all parts, laid end to end along the dimension named above; each array names one. Nothing has to cross between parts.
Inputs may be any that keep to these rules, and one draw needn't show every extreme that they name: `doc_lengths`: lengths sum to 8192; the longest is exactly 2048.
All inputs are finite; a program needn't handle non-finite values.
Results may differ from the reference program's by a relative error of at most 0.0038.
Values may be sent and summed in bfloat16 or wider, within the bound.
A program may use at most 320 MiB of HBM per device.

```python
import math
import jax
import jax.numpy as jnp
import numpy as np
from jax import lax

QUERY_HEADS = 32
KEY_VALUE_HEADS = 4
HEAD_SIZE = 128
TOK_DEV = 512
SPAN_DEV = 4
MOST_LEN = 2048
NDOCS = 8
WINDOW_TOKENS = 8192


def key_field(key):
    key_sample = jax.random.fold_in(key, 101)
    unscaled_keys = jnp.clip(jax.random.normal(key_sample, (WINDOW_TOKENS, KEY_VALUE_HEADS, HEAD_SIZE), jnp.float32), -6.0, 6.0)
    return unscaled_keys


def draw_keys(key, part):
    unscaled_keys = key_field(key)
    return unscaled_keys.reshape(WINDOW_TOKENS, KEY_VALUE_HEADS * HEAD_SIZE).astype(jnp.bfloat16)


def draw_queries(key, part):
    query_sample = jax.random.fold_in(key, 404)
    unscaled_queries = jnp.clip(jax.random.normal(query_sample, (WINDOW_TOKENS, KEY_VALUE_HEADS, QUERY_HEADS // KEY_VALUE_HEADS, HEAD_SIZE), jnp.float32), -6.0, 6.0)
    return unscaled_queries.reshape(WINDOW_TOKENS, QUERY_HEADS * HEAD_SIZE).astype(jnp.bfloat16)


def level_of(stream_key, shape, shards, smallest, largest):
    def one(axis_at, parts):
        heights = jax.random.uniform(jax.random.fold_in(jax.random.fold_in(stream_key, 6), axis_at), (parts,), jnp.float32, smallest / len(shards), largest / len(shards))
        return jnp.repeat(jnp.exp(heights), shape[axis_at] // parts).reshape((-1,) + (1,) * (len(shape) - axis_at - 1))

    factor_of = one(*shards[0])
    for cut in shards[1:]:
        factor_of = factor_of * one(*cut)
    return factor_of


def profile(number_of, total, bound, skew):
    loads = [(1 << 20) // math.isqrt(grade ** skew) + 1 for grade in range(2, number_of + 1)]
    surplus, holding = total - bound - (number_of - 1), [1] * (number_of - 1)
    while surplus > 0:
        movable = [i for i in range(number_of - 1) if holding[i] < bound]
        whole, left = sum([loads[i] for i in movable]), surplus
        for i in movable:
            more = min(bound - holding[i], max(1, left * loads[i] // whole), surplus)
            holding[i] = holding[i] + more
            surplus = surplus - more
    return np.array([bound] + holding)


def ragged(stream_key, number_of, total, reach, skew):
    if number_of == 2:
        one = jax.random.randint(stream_key, (), max(1, total - reach), min(reach, total - 1) + 1)
        return jnp.stack([one, total - one])
    lengths = jnp.asarray(profile(number_of, total, reach, skew), jnp.int32)
    couples = (number_of - 1) // 2
    source_of, taker = lengths[1:1 + 2 * couples:2], lengths[2:2 + 2 * couples:2]
    margin = jnp.minimum(source_of - 1, reach - taker)
    shifted = jax.random.randint(jax.random.fold_in(stream_key, 1), (couples,), 0, 1 << 20) % (margin + 1)
    lengths = lengths.at[1:1 + 2 * couples:2].set(source_of - shifted).at[2:2 + 2 * couples:2].set(taker + shifted)
    return lengths[jax.random.permutation(jax.random.fold_in(stream_key, 2), number_of)]


def centred(stream_key, dims, scale, reach, split=(), kind=jnp.bfloat16):
    array = jax.random.normal(stream_key, dims, jnp.float32) * scale
    if len(split) > 0:
        array = level_of(stream_key, dims, split, -0.22, 0.18) * array
    return jnp.clip(array, min=-reach, max=reach).astype(kind)


def setup_inputs(seed: int = 0, part: int = 0) -> dict:
    key_of = jax.random.split(jax.random.key(seed), 5)
    part_splits = jax.random.split(jax.random.fold_in(key_of[4], part), 5)
    return {
        "queries": draw_queries(jax.random.fold_in(jax.random.fold_in(key_of[4], part), 71), part),
        "keys": draw_keys(jax.random.fold_in(jax.random.fold_in(key_of[4], part), 71), part),
        "values": centred(part_splits[2], (WINDOW_TOKENS, KEY_VALUE_HEADS * HEAD_SIZE), 1.0, 6.0, ((0, 16),)),
        "doc_lengths": ragged(part_splits[3], NDOCS, WINDOW_TOKENS, MOST_LEN, 2).astype(jnp.int32),
    }


NEGATIVE = -1e30


def doc_index(positions, doc_ends):
    inside = (positions[:, None] >= doc_ends[None, :]).astype(jnp.int32)
    doc_count = jnp.sum(inside, axis=1).astype(jnp.int32)
    return jnp.where(positions >= 0, doc_count, -1).astype(jnp.int32)


def block_partial(query_matrix, key_matrix, value_matrix, allowed):
    row_total = query_matrix.shape[0]
    column_total = key_matrix.shape[0]
    grouped_heads = query_matrix.reshape(row_total, KEY_VALUE_HEADS, QUERY_HEADS // KEY_VALUE_HEADS, HEAD_SIZE).astype(jnp.float32)
    key_head_rows = key_matrix.reshape(column_total, KEY_VALUE_HEADS, HEAD_SIZE).astype(jnp.float32)
    value_head_rows = value_matrix.reshape(column_total, KEY_VALUE_HEADS, HEAD_SIZE).astype(jnp.float32)
    scores = jnp.einsum("rhgd,chd->rhgc", grouped_heads, key_head_rows) * (HEAD_SIZE ** -0.5)
    mask_wide = allowed[:, None, None, :]
    masked = jnp.where(mask_wide, scores, NEGATIVE)
    row_peak = jnp.max(masked, axis=3)
    weights = jnp.where(mask_wide, jnp.exp(masked - row_peak[..., None]), 0.0)
    weight_sum = jnp.sum(weights, axis=3)
    rounded = lax.optimization_barrier(weights.astype(jnp.bfloat16)).astype(jnp.float32)
    summed = jnp.einsum("rhgc,chd->rhgd", rounded, value_head_rows)
    return row_peak, weight_sum, summed


def combine(first, second):
    first_peak, first_sum, first_out = first
    second_peak, second_sum, second_out = second
    top_peak = jnp.maximum(first_peak, second_peak)
    first_scale = jnp.exp(first_peak - top_peak)
    second_scale = jnp.exp(second_peak - top_peak)
    return (top_peak, first_sum * first_scale + second_sum * second_scale,
            first_out * first_scale[..., None] + second_out * second_scale[..., None])


def reference(queries, keys, values, doc_lengths):
    doc_ends = jnp.cumsum(doc_lengths).astype(jnp.int32)
    blocks = queries.shape[0] // TOK_DEV
    offsets = jnp.arange(TOK_DEV, dtype=jnp.int32)

    def one_block(block_index):
        row_start = (block_index * TOK_DEV).astype(jnp.int32)
        query_matrix = lax.dynamic_slice_in_dim(queries, row_start, TOK_DEV, 0)
        query_pos = row_start + offsets
        query_doc = doc_index(query_pos, doc_ends)
        merged = None
        for distance in range(SPAN_DEV + 1):
            key_start = (row_start - distance * TOK_DEV).astype(jnp.int32)
            safe_start = jnp.maximum(key_start, 0).astype(jnp.int32)
            key_matrix = lax.dynamic_slice_in_dim(keys, safe_start, TOK_DEV, 0)
            value_matrix = lax.dynamic_slice_in_dim(values, safe_start, TOK_DEV, 0)
            key_pos = key_start + offsets
            key_doc = doc_index(key_pos, doc_ends)
            allowed = (query_doc[:, None] == key_doc[None, :]) & (key_pos[None, :] <= query_pos[:, None]) & (key_pos[None, :] >= 0)
            partial_value = block_partial(query_matrix, key_matrix, value_matrix, allowed)
            merged = partial_value if merged is None else combine(merged, partial_value)
        row_peak, weight_sum, summed = merged
        result = summed / weight_sum[..., None]
        return result.reshape(TOK_DEV, QUERY_HEADS * HEAD_SIZE).astype(jnp.bfloat16)

    output = lax.map(one_block, jnp.arange(blocks, dtype=jnp.int32))
    return output.reshape(queries.shape[0], QUERY_HEADS * HEAD_SIZE)
```

```python
import functools
import math

import jax
import jax.numpy as jnp
from jax import lax
from jax.experimental import pallas as pl
from jax.experimental.pallas import tpu as pltpu
from jax.sharding import PartitionSpec as P

QUERY_HEADS = 32
KEY_VALUE_HEADS = 4
HEAD_SIZE = 128
SPAN_DEV = 4
GROUP = QUERY_HEADS // KEY_VALUE_HEADS
TILE = 256
NEGATIVE = -1e30
SCALE = HEAD_SIZE ** (-0.5) * math.log2(math.e)


def from_behind(value, axis, steps):
    count = lax.axis_size(axis)
    initial, last = (max(0, -steps), min(count, count - steps))
    return lax.ppermute(value, axis, [(source, source + steps) for source in range(initial, last)])


def attend_tile(first_row, heads, query_of, store, row_bounds, kt, vx, scores, weights, reach):
    window = reach + TILE
    steps = window // TILE
    rows = lax.broadcasted_iota(jnp.int32, (TILE, HEAD_SIZE), 0) + first_row
    one_hot = ((rows >= row_bounds[0:1, :]) & (rows < row_bounds[1:2, :])).astype(jnp.float32)
    one_hot = one_hot.astype(jnp.bfloat16)
    causal = lax.broadcasted_iota(jnp.int32, (TILE, TILE), 1) <= lax.broadcasted_iota(
        jnp.int32, (TILE, TILE), 0
    )
    causal = jnp.concatenate([causal, causal], axis=0)
    tags = jnp.concatenate([one_hot, one_hot], axis=0)

    def pair(head, slot):
        both = jnp.concatenate([query_of(head), query_of(head + 1)], axis=0)
        left = jnp.concatenate([both, tags], axis=1)
        peak = None
        for step in range(steps):
            columns = pl.ds(pl.multiple_of(first_row + step * TILE, TILE), TILE)
            part = jnp.dot(left, kt[:, columns], preferred_element_type=jnp.float32)
            if step == steps - 1:
                part = jnp.where(causal, part, NEGATIVE)
            scores[slot, :, step * TILE : (step + 1) * TILE] = part
            high = jnp.maximum(part[:, :HEAD_SIZE], part[:, HEAD_SIZE:])
            peak = high if peak is None else jnp.maximum(peak, high)
        top = jnp.max(peak, axis=1, keepdims=True) * SCALE
        for step in range(steps):
            columns = slice(step * TILE, (step + 1) * TILE)
            weights[slot, :, columns] = jnp.exp2(scores[slot, :, columns] * SCALE - top).astype(
                jnp.bfloat16
            )
        keys_at = pl.ds(pl.multiple_of(first_row, TILE), window)
        total = jnp.dot(weights[slot], vx[keys_at, :], preferred_element_type=jnp.float32)
        result = (total[:, :HEAD_SIZE] / total[:, HEAD_SIZE:]).astype(jnp.bfloat16)
        store(head, result[:TILE])
        store(head + 1, result[TILE:])

    @pl.loop(0, heads // 4)
    def _(quad):
        for slot in range(2):
            pair(quad * 4 + slot * 2, slot)


def kernel(reach, *refs):
    blocks = SPAN_DEV + 1
    row_bounds, column_bounds, q = refs[:3]
    ks = refs[3 : 3 + blocks]
    vs = refs[3 + blocks : 3 + 2 * blocks]
    out, kt, vx, scores, weights = refs[3 + 2 * blocks :]
    group, tile = pl.program_id(0), pl.program_id(1)
    depth = ks[0].shape[0]

    @pl.when((group == 0) & (tile == 0))
    def _():
        place = lax.broadcasted_iota(jnp.int32, (HEAD_SIZE, TILE), 1) - reach
        for part in range(kt.shape[1] // TILE):
            at = place + part * TILE
            inside = (at >= column_bounds[:, 0:1]) & (at < column_bounds[:, 1:2])
            kt[HEAD_SIZE:, part * TILE : (part + 1) * TILE] = jnp.where(
                inside, 0.0, NEGATIVE
            ).astype(jnp.bfloat16)
        vx[:, HEAD_SIZE:] = jnp.ones((vx.shape[0], HEAD_SIZE), jnp.bfloat16)

    @pl.when(tile == 0)
    def _():
        for block in range(blocks):
            span = slice(block * depth, (block + 1) * depth)
            kt[:HEAD_SIZE, span] = ks[block][...].T
            vx[span, :HEAD_SIZE] = vs[block][...]

    def query_of(head):
        return q[:, pl.ds(pl.multiple_of(head * HEAD_SIZE, HEAD_SIZE), HEAD_SIZE)]

    def store(head, value):
        out[:, pl.ds(pl.multiple_of(head * HEAD_SIZE, HEAD_SIZE), HEAD_SIZE)] = value

    attend_tile(tile * TILE, GROUP, query_of, store, row_bounds, kt, vx, scores, weights, reach)


def body(queries, keys, values, doc_lengths):
    row_total = queries.shape[0]
    reach = SPAN_DEV * row_total
    start = lax.axis_index("ctx") * row_total
    docs = doc_lengths.shape[0]
    index = jnp.arange(HEAD_SIZE)
    lengths = jnp.zeros((HEAD_SIZE,), jnp.int32).at[:docs].set(doc_lengths)
    ends = jnp.sum(jnp.where(index[None, :] <= index[:, None], lengths[None, :], 0), axis=1)
    high = ends - start
    low = high - lengths
    row_bounds = jnp.concatenate([low[None], high[None], jnp.zeros((6, HEAD_SIZE), jnp.int32)])
    column_bounds = jnp.stack([low, high], axis=1)

    rows = jnp.concatenate([keys, values], axis=1)
    parts = [from_behind(rows, "ctx", distance) for distance in range(SPAN_DEV, 0, -1)] + [rows]
    wide = GROUP * HEAD_SIZE
    key_specs = [pl.BlockSpec((row_total, HEAD_SIZE), lambda g, t: (0, g)) for _ in parts]
    value_specs = [
        pl.BlockSpec((row_total, HEAD_SIZE), lambda g, t: (0, g + KEY_VALUE_HEADS)) for _ in parts
    ]
    whole = reach + row_total
    return pl.pallas_call(
        functools.partial(kernel, reach),
        grid=(KEY_VALUE_HEADS, row_total // TILE),
        out_shape=jax.ShapeDtypeStruct(queries.shape, jnp.bfloat16),
        in_specs=[
            pl.BlockSpec((8, HEAD_SIZE), lambda g, t: (0, 0)),
            pl.BlockSpec((HEAD_SIZE, 2), lambda g, t: (0, 0)),
            pl.BlockSpec((TILE, wide), lambda g, t: (t, g)),
        ]
        + key_specs
        + value_specs,
        out_specs=pl.BlockSpec((TILE, wide), lambda g, t: (t, g)),
        scratch_shapes=[
            pltpu.VMEM((2 * HEAD_SIZE, whole), jnp.bfloat16),
            pltpu.VMEM((whole, 2 * HEAD_SIZE), jnp.bfloat16),
            pltpu.VMEM((2, 2 * TILE, reach + TILE), jnp.float32),
            pltpu.VMEM((2, 2 * TILE, reach + TILE), jnp.bfloat16),
        ],
        compiler_params=pltpu.CompilerParams(vmem_limit_bytes=48 * 1024 * 1024),
    )(row_bounds, column_bounds, queries, *parts, *parts)


def solution(mesh):
    placed = (
        P(("groups", "ctx"), None),
        P(("groups", "ctx"), None),
        P(("groups", "ctx"), None),
        P("groups"),
    )
    return jax.shard_map(
        body, mesh=mesh, in_specs=placed, out_specs=P(("groups", "ctx"), None), check_vma=False
    )
```

```python
import functools
import math

import jax
import jax.numpy as jnp
from jax import lax
from jax.experimental import pallas as pl
from jax.experimental.pallas import tpu as pltpu
from jax.sharding import PartitionSpec as P

QUERY_HEADS = 32
KEY_VALUE_HEADS = 4
HEAD_SIZE = 128
SPAN_DEV = 4
GROUP = QUERY_HEADS // KEY_VALUE_HEADS
TILE = 256
NEGATIVE = -1e30
SCALE = HEAD_SIZE ** (-0.5) * math.log2(math.e)


def attend_tile(first_row, heads, query_of, store, row_bounds, kt, vx, scores, weights, reach):
    window = reach + TILE
    steps = window // TILE
    rows = lax.broadcasted_iota(jnp.int32, (TILE, HEAD_SIZE), 0) + first_row
    one_hot = ((rows >= row_bounds[0:1, :]) & (rows < row_bounds[1:2, :])).astype(jnp.float32)
    one_hot = one_hot.astype(jnp.bfloat16)
    causal = lax.broadcasted_iota(jnp.int32, (TILE, TILE), 1) <= lax.broadcasted_iota(
        jnp.int32, (TILE, TILE), 0
    )
    causal = jnp.concatenate([causal, causal], axis=0)
    tags = jnp.concatenate([one_hot, one_hot], axis=0)

    def scored(left, slot, step):
        columns = pl.ds(pl.multiple_of(first_row + step * TILE, TILE), TILE)
        part = jnp.dot(left, kt[:, columns], preferred_element_type=jnp.float32)
        if step == steps - 1:
            part = jnp.where(causal, part, NEGATIVE)
        scores[slot, :, step * TILE : (step + 1) * TILE] = part
        return jnp.maximum(part[:, :HEAD_SIZE], part[:, HEAD_SIZE:])

    def weighed(slot, step, top):
        columns = slice(step * TILE, (step + 1) * TILE)
        weights[slot, :, columns] = jnp.exp2(scores[slot, :, columns] * SCALE - top).astype(
            jnp.bfloat16
        )

    def left_of(pair):
        both = jnp.concatenate([query_of(2 * pair), query_of(2 * pair + 1)], axis=0)
        return jnp.concatenate([both, tags], axis=1)

    top = None
    pairs = heads // 2
    for pair in range(pairs + 1):
        slot, last = pair % 2, (pair + 1) % 2
        left = left_of(pair) if pair < pairs else None
        peak = None
        for step in range(steps):
            if pair < pairs:
                high = scored(left, slot, step)
                peak = high if peak is None else jnp.maximum(peak, high)
            if pair > 0:
                weighed(last, step, top)
        if pair < pairs:
            top = jnp.max(peak, axis=1, keepdims=True) * SCALE
        if pair > 0:
            keys_at = pl.ds(pl.multiple_of(first_row, TILE), window)
            total = jnp.dot(weights[last], vx[keys_at, :], preferred_element_type=jnp.float32)
            result = (total[:, :HEAD_SIZE] / total[:, HEAD_SIZE:]).astype(jnp.bfloat16)
            store(2 * pair - 2, result[:TILE])
            store(2 * pair - 1, result[TILE:])


def transfers(keys, values, land, send_sem, recv_sem):
    count = lax.axis_size("ctx")
    me = lax.axis_index("ctx")
    core, odd = me % 2, (me // 2) % 2
    ahead, behind = (me + SPAN_DEV) % count, (me + count - SPAN_DEV) % count
    across = me + 2 - 4 * odd
    partner = me + 1 - 2 * core
    own = (keys, values)

    def copy(source, slot, head, kind, target):
        return pltpu.make_async_remote_copy(
            src_ref=source,
            dst_ref=land.at[slot, kind, head],
            send_sem=send_sem.at[slot, kind, head],
            recv_sem=recv_sem.at[slot, kind, head],
            device_id={"ctx": target},
            device_id_type=pl.DeviceIdType.MESH,
        )

    def mine(head, kind):
        return own[kind].at[:, head * HEAD_SIZE : (head + 1) * HEAD_SIZE]

    def both(action):
        for kind in range(2):
            action(kind)

    def begin():
        barrier = pltpu.get_barrier_semaphore()
        for other in (ahead, behind, across, partner):
            pl.semaphore_signal(
                barrier, inc=1, device_id={"ctx": other}, device_id_type=pl.DeviceIdType.MESH
            )
        pl.semaphore_wait(barrier, 4)
        for head in range(KEY_VALUE_HEADS):
            both(lambda kind: copy(mine(head, kind), 3, head, kind, ahead).start())

            @pl.when(odd == 0)
            def _():
                both(lambda kind: copy(mine(head, kind), 1, head, kind, across).start())

            @pl.when(core == 0)
            def _():
                both(lambda kind: copy(mine(head, kind), 0, head, kind, partner).start())

    def far(head):
        both(lambda kind: copy(mine(head, kind), 3, head, kind, ahead).wait_recv())

        @pl.when(odd == 1)
        def _():
            both(lambda kind: copy(land.at[3, kind, head], 1, head, kind, across).start())

        @pl.when(core == 1)
        def _():
            both(lambda kind: copy(land.at[3, kind, head], 2, head, kind, partner).start())

    def near(head):
        both(lambda kind: copy(mine(head, kind), 1, head, kind, across).wait_recv())

        @pl.when(core == 0)
        def _():
            both(lambda kind: copy(land.at[1, kind, head], 2, head, kind, partner).start())

        @pl.when(core == 1)
        def _():
            both(lambda kind: copy(land.at[1, kind, head], 0, head, kind, partner).start())

    def beside(head):
        for slot in (0, 2):
            both(lambda kind: copy(mine(head, kind), slot, head, kind, partner).wait_recv())

    def finish():
        for head in range(KEY_VALUE_HEADS):
            for slot in range(SPAN_DEV):
                both(lambda kind: copy(mine(head, kind), slot, head, kind, ahead).wait_send())

    return begin, far, near, beside, finish


def kernel(lengths, keys, values, q, out, row_bounds, land, kt, vx, scores, weights, send_sem, recv_sem):
    group, tile = pl.program_id(0), pl.program_id(1)
    groups, tiles = KEY_VALUE_HEADS, q_tiles(keys)
    depth = keys.shape[0]
    reach = SPAN_DEV * depth
    begin, far, near, beside, finish = transfers(keys, values, land, send_sem, recv_sem)

    @pl.when((group == 0) & (tile == 0))
    def _():
        begin()
        lane = lax.broadcasted_iota(jnp.int32, (8, HEAD_SIZE), 1)
        line = lax.broadcasted_iota(jnp.int32, (HEAD_SIZE, TILE), 0)
        row_low = row_high = jnp.zeros((8, HEAD_SIZE), jnp.int32)
        low = high = jnp.zeros((HEAD_SIZE, TILE), jnp.int32)
        first = -lax.axis_index("ctx") * depth
        for doc in range(lengths.shape[0]):
            last = first + lengths[doc]
            row_low, row_high = jnp.where(lane == doc, first, row_low), jnp.where(lane == doc, last, row_high)
            low, high = jnp.where(line == doc, first, low), jnp.where(line == doc, last, high)
            first = last
        row_bounds[0], row_bounds[1] = row_low, row_high
        place = lax.broadcasted_iota(jnp.int32, (HEAD_SIZE, TILE), 1) - reach
        for part in range(kt.shape[1] // TILE):
            at = place + part * TILE
            kt[HEAD_SIZE:, part * TILE : (part + 1) * TILE] = jnp.where(
                (at >= low) & (at < high), 0.0, NEGATIVE
            ).astype(jnp.bfloat16)
        vx[:, HEAD_SIZE:] = jnp.ones((vx.shape[0], HEAD_SIZE), jnp.bfloat16)

    for head in range(groups):

        @pl.when((group == head) & (tile == 0))
        def _():
            if head == 0:
                far(0)
                near(0)
                far(1)
            beside(head)
            span = slice(reach, reach + depth)
            columns = slice(head * HEAD_SIZE, (head + 1) * HEAD_SIZE)
            kt[:HEAD_SIZE, span] = keys[:, columns].T
            vx[span, :HEAD_SIZE] = values[:, columns]

        if head + 1 < groups:

            @pl.when((group == head) & (tile == tiles - 1))
            def _():
                near(head + 1)
                if head + 2 < groups:
                    far(head + 2)

    @pl.when(tile == 0)
    def _():
        for slot in range(SPAN_DEV):
            span = slice(reach - (slot + 1) * depth, reach - slot * depth)
            kt[:HEAD_SIZE, span] = land[slot, 0, group].T
            vx[span, :HEAD_SIZE] = land[slot, 1, group]

    def query_of(head):
        return q[:, head * HEAD_SIZE : (head + 1) * HEAD_SIZE]

    def store(head, value):
        out[:, head * HEAD_SIZE : (head + 1) * HEAD_SIZE] = value

    bounds = jnp.concatenate([row_bounds[0][:1], row_bounds[1][:1]], axis=0)
    attend_tile(tile * TILE, GROUP, query_of, store, bounds, kt, vx, scores, weights, reach)

    @pl.when((group == groups - 1) & (tile == tiles - 1))
    def _():
        finish()


def q_tiles(keys):
    return keys.shape[0] // TILE


def body(queries, keys, values, doc_lengths):
    row_total = queries.shape[0]
    reach = SPAN_DEV * row_total
    wide = GROUP * HEAD_SIZE
    whole = reach + row_total
    travel = (SPAN_DEV, 2, KEY_VALUE_HEADS)
    return pl.pallas_call(
        kernel,
        grid=(KEY_VALUE_HEADS, row_total // TILE),
        out_shape=jax.ShapeDtypeStruct(queries.shape, jnp.bfloat16),
        in_specs=[
            pl.BlockSpec(memory_space=pltpu.SMEM),
            pl.BlockSpec(memory_space=pltpu.VMEM),
            pl.BlockSpec(memory_space=pltpu.VMEM),
            pl.BlockSpec((TILE, wide), lambda g, t: (t, g)),
        ],
        out_specs=pl.BlockSpec((TILE, wide), lambda g, t: (t, g)),
        scratch_shapes=[
            pltpu.VMEM((2, 8, HEAD_SIZE), jnp.int32),
            pltpu.VMEM(travel + (row_total, HEAD_SIZE), jnp.bfloat16),
            pltpu.VMEM((2 * HEAD_SIZE, whole), jnp.bfloat16),
            pltpu.VMEM((whole, 2 * HEAD_SIZE), jnp.bfloat16),
            pltpu.VMEM((2, 2 * TILE, reach + TILE), jnp.float32),
            pltpu.VMEM((2, 2 * TILE, reach + TILE), jnp.bfloat16),
            pltpu.SemaphoreType.DMA(travel),
            pltpu.SemaphoreType.DMA(travel),
        ],
        compiler_params=pltpu.CompilerParams(
            vmem_limit_bytes=48 * 1024 * 1024, collective_id=0, has_side_effects=True
        ),
    )(doc_lengths, keys, values, queries)


def solution(mesh):
    placed = (
        P(("groups", "ctx"), None),
        P(("groups", "ctx"), None),
        P(("groups", "ctx"), None),
        P("groups"),
    )
    return jax.shard_map(
        body, mesh=mesh, in_specs=placed, out_specs=P(("groups", "ctx"), None), check_vma=False
    )
```

```python
import functools
import math

import jax
import jax.numpy as jnp
from jax import lax
from jax.experimental import pallas as pl
from jax.experimental.pallas import tpu as pltpu
from jax.sharding import PartitionSpec as P

QUERY_HEADS = 32
KEY_VALUE_HEADS = 4
HEAD_SIZE = 128
SPAN_DEV = 4
GROUP = QUERY_HEADS // KEY_VALUE_HEADS
TILE = 256
NEGATIVE = -1e30
SCALE = HEAD_SIZE ** (-0.5) * math.log2(math.e)


def attend_tile(first_row, heads, query_of, store, row_bounds, kt, vx, scores, weights, reach):
    window = reach + TILE
    steps = window // TILE
    rows = lax.broadcasted_iota(jnp.int32, (TILE, HEAD_SIZE), 0) + first_row
    one_hot = ((rows >= row_bounds[0:1, :]) & (rows < row_bounds[1:2, :])).astype(jnp.float32)
    one_hot = one_hot.astype(jnp.bfloat16)
    causal = lax.broadcasted_iota(jnp.int32, (TILE, TILE), 1) <= lax.broadcasted_iota(
        jnp.int32, (TILE, TILE), 0
    )
    causal = jnp.concatenate([causal, causal], axis=0)
    tags = jnp.concatenate([one_hot, one_hot], axis=0)

    def scored(left, slot, step):
        columns = pl.ds(pl.multiple_of(first_row + step * TILE, TILE), TILE)
        part = jnp.dot(left, kt[:, columns], preferred_element_type=jnp.float32)
        if step == steps - 1:
            part = jnp.where(causal, part, NEGATIVE)
        scores[slot, :, step * TILE : (step + 1) * TILE] = part
        return jnp.maximum(part[:, :HEAD_SIZE], part[:, HEAD_SIZE:])

    def weighed(slot, step, top):
        columns = slice(step * TILE, (step + 1) * TILE)
        weights[slot, :, columns] = jnp.exp2((scores[slot, :, columns] - top) * SCALE).astype(
            jnp.bfloat16
        )

    def left_of(pair):
        both = jnp.concatenate([query_of(2 * pair), query_of(2 * pair + 1)], axis=0)
        return jnp.concatenate([both, tags], axis=1)

    top = None
    pairs = heads // 2
    for pair in range(pairs + 1):
        slot, last = pair % 2, (pair + 1) % 2
        left = left_of(pair) if pair < pairs else None
        peak = None
        for step in range(steps):
            if pair < pairs:
                high = scored(left, slot, step)
                peak = high if peak is None else jnp.maximum(peak, high)
            if pair > 0:
                weighed(last, step, top)
        if pair < pairs:
            top = jnp.max(peak, axis=1, keepdims=True)
        if pair > 0:
            keys_at = pl.ds(pl.multiple_of(first_row, TILE), window)
            total = jnp.dot(weights[last], vx[keys_at, :], preferred_element_type=jnp.float32)
            result = (total[:, :HEAD_SIZE] * pl.reciprocal(total[:, HEAD_SIZE:])).astype(jnp.bfloat16)
            store(2 * pair - 2, result[:TILE])
            store(2 * pair - 1, result[TILE:])


def transfers(keys, values, land, send_sem, recv_sem):
    count = lax.axis_size("ctx")
    me = lax.axis_index("ctx")
    core, odd = me % 2, (me // 2) % 2
    ahead, behind = (me + SPAN_DEV) % count, (me + count - SPAN_DEV) % count
    across = me + 2 - 4 * odd
    partner = me + 1 - 2 * core
    own = (keys, values)

    def copy(source, slot, head, kind, target):
        return pltpu.make_async_remote_copy(
            src_ref=source,
            dst_ref=land.at[slot, kind, head],
            send_sem=send_sem.at[slot, kind, head],
            recv_sem=recv_sem.at[slot, kind, head],
            device_id={"ctx": target},
            device_id_type=pl.DeviceIdType.MESH,
        )

    def mine(head, kind):
        return own[kind].at[:, head * HEAD_SIZE : (head + 1) * HEAD_SIZE]

    def both(action):
        for kind in range(2):
            action(kind)

    def begin():
        barrier = pltpu.get_barrier_semaphore()
        for other in (ahead, behind, across, partner):
            pl.semaphore_signal(
                barrier, inc=1, device_id={"ctx": other}, device_id_type=pl.DeviceIdType.MESH
            )
        pl.semaphore_wait(barrier, 4)
        for head in range(KEY_VALUE_HEADS):
            both(lambda kind: copy(mine(head, kind), 3, head, kind, ahead).start())

            @pl.when(odd == 0)
            def _():
                both(lambda kind: copy(mine(head, kind), 1, head, kind, across).start())

            @pl.when(core == 0)
            def _():
                both(lambda kind: copy(mine(head, kind), 0, head, kind, partner).start())

    def far(head):
        for kind in range(2):
            copy(mine(head, kind), 3, head, kind, ahead).wait_recv()

            @pl.when(odd == 1)
            def _():
                copy(land.at[3, kind, head], 1, head, kind, across).start()

            @pl.when(core == 1)
            def _():
                copy(land.at[3, kind, head], 2, head, kind, partner).start()

    def near(head):
        for kind in range(2):
            copy(mine(head, kind), 1, head, kind, across).wait_recv()

            @pl.when(core == 0)
            def _():
                copy(land.at[1, kind, head], 2, head, kind, partner).start()

            @pl.when(core == 1)
            def _():
                copy(land.at[1, kind, head], 0, head, kind, partner).start()

    def beside(head):
        for slot in (0, 2):
            both(lambda kind: copy(mine(head, kind), slot, head, kind, partner).wait_recv())

    def finish():
        for head in range(KEY_VALUE_HEADS):
            for slot in range(SPAN_DEV):
                both(lambda kind: copy(mine(head, kind), slot, head, kind, ahead).wait_send())

    return begin, far, near, beside, finish


def kernel(lengths, keys, values, q, out, row_bounds, land, kt, vx, scores, weights, send_sem, recv_sem):
    group, tile = pl.program_id(0), pl.program_id(1)
    groups, tiles = KEY_VALUE_HEADS, q_tiles(keys)
    depth = keys.shape[0]
    reach = SPAN_DEV * depth
    begin, far, near, beside, finish = transfers(keys, values, land, send_sem, recv_sem)

    @pl.when((group == 0) & (tile == 0))
    def _():
        begin()
        lane = lax.broadcasted_iota(jnp.int32, (8, HEAD_SIZE), 1)
        line = lax.broadcasted_iota(jnp.int32, (HEAD_SIZE, TILE), 0)
        row_low = row_high = jnp.zeros((8, HEAD_SIZE), jnp.int32)
        low = high = jnp.zeros((HEAD_SIZE, TILE), jnp.int32)
        first = -lax.axis_index("ctx") * depth
        for doc in range(lengths.shape[0]):
            last = first + lengths[doc]
            row_low, row_high = jnp.where(lane == doc, first, row_low), jnp.where(lane == doc, last, row_high)
            low, high = jnp.where(line == doc, first, low), jnp.where(line == doc, last, high)
            first = last
        row_bounds[0], row_bounds[1] = row_low, row_high
        place = lax.broadcasted_iota(jnp.int32, (HEAD_SIZE, TILE), 1) - reach
        for part in range(kt.shape[1] // TILE):
            at = place + part * TILE
            kt[HEAD_SIZE:, part * TILE : (part + 1) * TILE] = jnp.where(
                (at >= low) & (at < high), 0.0, NEGATIVE
            ).astype(jnp.bfloat16)
        vx[:, HEAD_SIZE:] = jnp.ones((vx.shape[0], HEAD_SIZE), jnp.bfloat16)

    def fill(slot, head):
        span = slice(reach - (slot + 1) * depth, reach - slot * depth)
        kt[:HEAD_SIZE, span] = land[slot, 0, head].T
        vx[span, :HEAD_SIZE] = land[slot, 1, head]

    for head in range(groups):

        @pl.when((group == head) & (tile == 0))
        def _():
            span = slice(reach, reach + depth)
            columns = slice(head * HEAD_SIZE, (head + 1) * HEAD_SIZE)
            kt[:HEAD_SIZE, span] = keys[:, columns].T
            vx[span, :HEAD_SIZE] = values[:, columns]
            if head == 0:
                far(0)
            fill(3, head)
            if head == 0:
                near(0)
            fill(1, head)
            beside(head)
            if head == 0:
                far(1)
            fill(0, head)
            fill(2, head)

        if head + 1 < groups:

            @pl.when((group == head) & (tile == tiles - 1))
            def _():
                near(head + 1)
                if head + 2 < groups:
                    far(head + 2)

    def query_of(head):
        return q[:, head * HEAD_SIZE : (head + 1) * HEAD_SIZE]

    def store(head, value):
        out[:, head * HEAD_SIZE : (head + 1) * HEAD_SIZE] = value

    bounds = jnp.concatenate([row_bounds[0][:1], row_bounds[1][:1]], axis=0)
    attend_tile(tile * TILE, GROUP, query_of, store, bounds, kt, vx, scores, weights, reach)

    @pl.when((group == groups - 1) & (tile == tiles - 1))
    def _():
        finish()


def q_tiles(keys):
    return keys.shape[0] // TILE


def body(queries, keys, values, doc_lengths):
    row_total = queries.shape[0]
    reach = SPAN_DEV * row_total
    wide = GROUP * HEAD_SIZE
    whole = reach + row_total
    travel = (SPAN_DEV, 2, KEY_VALUE_HEADS)
    return pl.pallas_call(
        kernel,
        grid=(KEY_VALUE_HEADS, row_total // TILE),
        out_shape=jax.ShapeDtypeStruct(queries.shape, jnp.bfloat16),
        in_specs=[
            pl.BlockSpec(memory_space=pltpu.SMEM),
            pl.BlockSpec(keys.shape, lambda g, t: (0, 0)),
            pl.BlockSpec(values.shape, lambda g, t: (0, 0)),
            pl.BlockSpec((TILE, wide), lambda g, t: (t, g)),
        ],
        out_specs=pl.BlockSpec((TILE, wide), lambda g, t: (t, g)),
        scratch_shapes=[
            pltpu.VMEM((2, 8, HEAD_SIZE), jnp.int32),
            pltpu.VMEM(travel + (row_total, HEAD_SIZE), jnp.bfloat16),
            pltpu.VMEM((2 * HEAD_SIZE, whole), jnp.bfloat16),
            pltpu.VMEM((whole, 2 * HEAD_SIZE), jnp.bfloat16),
            pltpu.VMEM((2, 2 * TILE, reach + TILE), jnp.float32),
            pltpu.VMEM((2, 2 * TILE, reach + TILE), jnp.bfloat16),
            pltpu.SemaphoreType.DMA(travel),
            pltpu.SemaphoreType.DMA(travel),
        ],
        compiler_params=pltpu.CompilerParams(
            vmem_limit_bytes=48 * 1024 * 1024, collective_id=0, has_side_effects=True
        ),
    )(doc_lengths, keys, values, queries)


def solution(mesh):
    placed = (
        P(("groups", "ctx"), None),
        P(("groups", "ctx"), None),
        P(("groups", "ctx"), None),
        P("groups"),
    )
    return jax.shard_map(
        body, mesh=mesh, in_specs=placed, out_specs=P(("groups", "ctx"), None), check_vma=False
    )
```

```python
import functools
import math

import jax
import jax.numpy as jnp
from jax import lax
from jax.experimental import pallas as pl
from jax.experimental.pallas import tpu as pltpu
from jax.sharding import PartitionSpec as P

QUERY_HEADS = 32
KEY_VALUE_HEADS = 4
HEAD_SIZE = 128
SPAN_DEV = 4
GROUP = QUERY_HEADS // KEY_VALUE_HEADS
TILE = 256
NEGATIVE = -1e30
SCALE = HEAD_SIZE ** (-0.5) * math.log2(math.e)


def attend_tile(first_row, heads, query_of, store, row_bounds, kt, vx, scores, weights, reach):
    window = reach + TILE
    steps = window // TILE
    rows = lax.broadcasted_iota(jnp.int32, (TILE, HEAD_SIZE), 0) + first_row
    one_hot = ((rows >= row_bounds[0:1, :]) & (rows < row_bounds[1:2, :])).astype(jnp.float32)
    one_hot = one_hot.astype(jnp.bfloat16)
    causal = lax.broadcasted_iota(jnp.int32, (TILE, TILE), 1) <= lax.broadcasted_iota(
        jnp.int32, (TILE, TILE), 0
    )
    causal = jnp.concatenate([causal, causal], axis=0)
    tags = jnp.concatenate([one_hot, one_hot], axis=0)

    def scored(left, slot, step):
        columns = pl.ds(pl.multiple_of(first_row + step * TILE, TILE), TILE)
        part = jnp.dot(left, kt[:, columns], preferred_element_type=jnp.float32)
        if step == steps - 1:
            part = jnp.where(causal, part, NEGATIVE)
        scores[slot, :, step * TILE : (step + 1) * TILE] = part
        return jnp.maximum(part[:, :HEAD_SIZE], part[:, HEAD_SIZE:])

    def weighed(slot, step, top):
        columns = slice(step * TILE, (step + 1) * TILE)
        weights[slot, :, columns] = jnp.exp2((scores[slot, :, columns] - top) * SCALE).astype(
            jnp.bfloat16
        )

    def left_of(pair):
        both = jnp.concatenate([query_of(2 * pair), query_of(2 * pair + 1)], axis=0)
        return jnp.concatenate([both, tags], axis=1)

    top = None
    pairs = heads // 2
    for pair in range(pairs + 1):
        slot, last = pair % 2, (pair + 1) % 2
        left = left_of(pair) if pair < pairs else None
        peak = None
        for step in range(steps):
            if pair < pairs:
                high = scored(left, slot, step)
                peak = high if peak is None else jnp.maximum(peak, high)
            if pair > 0:
                weighed(last, step, top)
        if pair < pairs:
            top = jnp.max(peak, axis=1, keepdims=True)
        if pair > 0:
            keys_at = pl.ds(pl.multiple_of(first_row, TILE), window)
            total = jnp.dot(weights[last], vx[keys_at, :], preferred_element_type=jnp.float32)
            result = (total[:, :HEAD_SIZE] * pl.reciprocal(total[:, HEAD_SIZE:])).astype(jnp.bfloat16)
            store(2 * pair - 2, result[:TILE])
            store(2 * pair - 1, result[TILE:])


def transfers(keys, values, land, send_sem, recv_sem):
    count = lax.axis_size("ctx")
    me = lax.axis_index("ctx")
    core, odd = me % 2, (me // 2) % 2
    ahead, behind = (me + SPAN_DEV) % count, (me + count - SPAN_DEV) % count
    across = me + 2 - 4 * odd
    partner = me + 1 - 2 * core
    own = (keys, values)

    def copy(source, slot, head, kind, target):
        return pltpu.make_async_remote_copy(
            src_ref=source,
            dst_ref=land.at[slot, kind, head],
            send_sem=send_sem.at[slot, kind, head],
            recv_sem=recv_sem.at[slot, kind, head],
            device_id={"ctx": target},
            device_id_type=pl.DeviceIdType.MESH,
        )

    def mine(head, kind):
        return own[kind].at[:, head * HEAD_SIZE : (head + 1) * HEAD_SIZE]

    def both(action):
        for kind in range(2):
            action(kind)

    def begin():
        barrier = pltpu.get_barrier_semaphore()
        for other in (ahead, behind, across, partner):
            pl.semaphore_signal(
                barrier, inc=1, device_id={"ctx": other}, device_id_type=pl.DeviceIdType.MESH
            )
        pl.semaphore_wait(barrier, 4)
        for head in range(KEY_VALUE_HEADS):
            both(lambda kind: copy(mine(head, kind), 3, head, kind, ahead).start())

            @pl.when(odd == 0)
            def _():
                both(lambda kind: copy(mine(head, kind), 1, head, kind, across).start())

            @pl.when(core == 0)
            def _():
                both(lambda kind: copy(mine(head, kind), 0, head, kind, partner).start())

    def far(head):
        for kind in range(2):
            copy(mine(head, kind), 3, head, kind, ahead).wait_recv()

            @pl.when(odd == 1)
            def _():
                copy(land.at[3, kind, head], 1, head, kind, across).start()

            @pl.when(core == 1)
            def _():
                copy(land.at[3, kind, head], 2, head, kind, partner).start()

    def near(head):
        for kind in range(2):
            copy(mine(head, kind), 1, head, kind, across).wait_recv()

            @pl.when(core == 0)
            def _():
                copy(land.at[1, kind, head], 2, head, kind, partner).start()

            @pl.when(core == 1)
            def _():
                copy(land.at[1, kind, head], 0, head, kind, partner).start()

    def beside(head):
        for slot in (0, 2):
            both(lambda kind: copy(mine(head, kind), slot, head, kind, partner).wait_recv())

    def finish():
        for head in range(KEY_VALUE_HEADS):
            for slot in range(SPAN_DEV):
                both(lambda kind: copy(mine(head, kind), slot, head, kind, ahead).wait_send())

    return begin, far, near, beside, finish


def kernel(lengths, keys, values, q, out, row_bounds, land, kt, vx, scores, weights, send_sem, recv_sem):
    group, tile = pl.program_id(0), pl.program_id(1)
    groups, tiles = KEY_VALUE_HEADS, q_tiles(keys)
    depth = keys.shape[0]
    reach = SPAN_DEV * depth
    begin, far, near, beside, finish = transfers(keys, values, land, send_sem, recv_sem)

    @pl.when((group == 0) & (tile == 0))
    def _():
        begin()
        lane = lax.broadcasted_iota(jnp.int32, (8, HEAD_SIZE), 1)
        line = lax.broadcasted_iota(jnp.int32, (HEAD_SIZE, TILE), 0)
        row_low = row_high = jnp.zeros((8, HEAD_SIZE), jnp.int32)
        low = high = jnp.zeros((HEAD_SIZE, TILE), jnp.int32)
        first = -lax.axis_index("ctx") * depth
        for doc in range(lengths.shape[0]):
            last = first + lengths[doc]
            row_low, row_high = jnp.where(lane == doc, first, row_low), jnp.where(lane == doc, last, row_high)
            low, high = jnp.where(line == doc, first, low), jnp.where(line == doc, last, high)
            first = last
        row_bounds[0], row_bounds[1] = row_low, row_high
        place = lax.broadcasted_iota(jnp.int32, (HEAD_SIZE, TILE), 1) - reach
        for part in range(kt.shape[1] // TILE):
            at = place + part * TILE
            kt[HEAD_SIZE:, part * TILE : (part + 1) * TILE] = jnp.where(
                (at >= low) & (at < high), 0.0, NEGATIVE
            ).astype(jnp.bfloat16)
        vx[:, HEAD_SIZE:] = jnp.ones((vx.shape[0], HEAD_SIZE), jnp.bfloat16)

    def fill(slot, head):
        span = slice(reach - (slot + 1) * depth, reach - slot * depth)
        kt[:HEAD_SIZE, span] = land[slot, 0, head].T
        vx[span, :HEAD_SIZE] = land[slot, 1, head]

    for head in range(groups):

        @pl.when((group == head) & (tile == 0))
        def _():
            span = slice(reach, reach + depth)
            columns = slice(head * HEAD_SIZE, (head + 1) * HEAD_SIZE)
            kt[:HEAD_SIZE, span] = keys[:, columns].T
            vx[span, :HEAD_SIZE] = values[:, columns]
            if head == 0:
                far(0)
            fill(3, head)
            if head == 0:
                near(0)
            fill(1, head)
            beside(head)
            if head == 0:
                far(1)
            fill(0, head)
            fill(2, head)

        if head + 1 < groups:

            @pl.when((group == head) & (tile == tiles - 1))
            def _():
                near(head + 1)
                if head + 2 < groups:
                    far(head + 2)

    def query_of(head):
        return q[:, head * HEAD_SIZE : (head + 1) * HEAD_SIZE]

    def store(head, value):
        out[:, head * HEAD_SIZE : (head + 1) * HEAD_SIZE] = value

    bounds = jnp.concatenate([row_bounds[0][:1], row_bounds[1][:1]], axis=0)
    attend_tile(tile * TILE, GROUP, query_of, store, bounds, kt, vx, scores, weights, reach)

    @pl.when((group == groups - 1) & (tile == tiles - 1))
    def _():
        finish()


def q_tiles(keys):
    return keys.shape[0] // TILE


def body(queries, keys, values, doc_lengths):
    row_total = queries.shape[0]
    reach = SPAN_DEV * row_total
    wide = GROUP * HEAD_SIZE
    whole = reach + row_total
    travel = (SPAN_DEV, 2, KEY_VALUE_HEADS)
    return pl.pallas_call(
        kernel,
        grid=(KEY_VALUE_HEADS, row_total // TILE),
        out_shape=jax.ShapeDtypeStruct(queries.shape, jnp.bfloat16),
        in_specs=[
            pl.BlockSpec(memory_space=pltpu.SMEM),
            pl.BlockSpec(keys.shape, lambda g, t: (0, 0)),
            pl.BlockSpec(values.shape, lambda g, t: (0, 0)),
            pl.BlockSpec((TILE, wide), lambda g, t: (t, g)),
        ],
        out_specs=pl.BlockSpec((TILE, wide), lambda g, t: (t, g)),
        scratch_shapes=[
            pltpu.VMEM((2, 8, HEAD_SIZE), jnp.int32),
            pltpu.VMEM(travel + (row_total, HEAD_SIZE), jnp.bfloat16),
            pltpu.VMEM((2 * HEAD_SIZE, whole), jnp.bfloat16),
            pltpu.VMEM((whole, 2 * HEAD_SIZE), jnp.bfloat16),
            pltpu.VMEM((2, 2 * TILE, reach + TILE), jnp.float32),
            pltpu.VMEM((2, 2 * TILE, reach + TILE), jnp.bfloat16),
            pltpu.SemaphoreType.DMA(travel),
            pltpu.SemaphoreType.DMA(travel),
        ],
        compiler_params=pltpu.CompilerParams(
            vmem_limit_bytes=67043328, collective_id=0, has_side_effects=True
        ),
    )(doc_lengths, keys, values, queries)


def solution(mesh):
    placed = (
        P(("groups", "ctx"), None),
        P(("groups", "ctx"), None),
        P(("groups", "ctx"), None),
        P("groups"),
    )
    return jax.shard_map(
        body, mesh=mesh, in_specs=placed, out_specs=P(("groups", "ctx"), None), check_vma=False
    )
```
